32 devices in a mesh: tm: 4 (over y, x), space: 8 (over z, core).
Axes of the slice: x: 2, y: 2, z: 4, core: 2. Of those that a mesh axis runs over, the one named last changes fastest.
Arguments:
- queries: bfloat16 [4, 768, 3072], P('tm', 'space'), may hold values from -8 to 8
- key_rows: bfloat16 [4, 768, 3072], P('tm', 'space'), may hold values from -8 to 8
- value_rows: bfloat16 [4, 768, 3072], P('tm', 'space'), may hold values from -6 to 6
- noise_level: int32 [4], P('tm'), may hold values from 0 to 999
- decay_power: int32 [24], replicated, may hold values from 0 to 7
- head_gain: float32 [24, 128], replicated, may hold values from 0.1 to 1.9
Outputs:
- attended: bfloat16 [4, 768, 3072], P('tm', 'space')
The draws below stay inside these ranges and needn't reach their ends.
All inputs are finite; a program needn't handle non-finite values.
Results may differ from the reference program's by a relative error of at most 0.0049.
Values may be sent and summed in bfloat16 or wider, within the bound.
A program may use at most 64 MiB of HBM per device.

```python
import jax
import jax.numpy as jnp
from jax import lax

HEADS = 24
HD = 128
LEVELS = 1000
BLOCKS = 4
TOK_BLK = 768


def draw_entries(key):
    extent = (BLOCKS, TOK_BLK, HEADS * HD)
    query_key = jax.random.fold_in(key, 11)
    keys_key = jax.random.fold_in(key, 12)
    queries = jax.random.truncated_normal(query_key, -8.0, 8.0, extent, jnp.float32)
    keys_all = jax.random.truncated_normal(keys_key, -8.0, 8.0, extent, jnp.float32)
    return (queries, keys_all)


def draw_queries(key, part):
    return draw_entries(key)[0].astype(jnp.bfloat16)


def draw_key_rows(key, part):
    return draw_entries(key)[1].astype(jnp.bfloat16)


def touch_ends(array, stream_key, smallest, high):
    longest = array.shape.index(max(array.shape))
    spots = []
    for shift in (0, 1):
        where = [jax.random.randint(jax.random.fold_in(stream_key, axis), (), 0, length) for axis, length in enumerate(array.shape)]
        where[longest] = (where[longest] + shift) % array.shape[longest]
        spots.append(tuple(where))
    return array.at[spots[0]].set(smallest).at[spots[1]].set(high)


def block_scale(key, shape, pieces, least, high):
    def one(position, shards_of):
        heights = jax.random.uniform(jax.random.fold_in(jax.random.fold_in(key, 6), position), (shards_of,), jnp.float32, least / len(pieces), high / len(pieces))
        return jnp.repeat(jnp.exp(heights), shape[position] // shards_of).reshape((-1,) + (1,) * (len(shape) - position - 1))

    loudness = one(*pieces[0])
    for cut in pieces[1:]:
        loudness = loudness * one(*cut)
    return loudness


def gaussian(key, shape, scale, reach, shards=(), held_as=jnp.bfloat16):
    level = block_scale(key, shape, shards, -0.22, 0.18) if shards else 1.0
    entries = jax.random.normal(key, shape, jnp.float32) * scale * level
    return jnp.minimum(jnp.maximum(entries, -reach), reach).astype(held_as)


def setup_inputs(seed: int = 0) -> dict:
    key_list = jax.random.split(jax.random.key(seed), 7)
    return {
        "queries": draw_queries(jax.random.fold_in(key_list[6], 71), 0),
        "key_rows": draw_key_rows(jax.random.fold_in(key_list[6], 71), 0),
        "value_rows": gaussian(key_list[2], (BLOCKS, TOK_BLK, HEADS * HD), 1.0, 6.0, ((0, 4), (1, 8))),
        "noise_level": touch_ends(jax.random.randint(key_list[3], (BLOCKS,), 0, LEVELS), jax.random.fold_in(key_list[3], 1), 0, LEVELS - 1).astype(jnp.int32),
        "decay_power": touch_ends(jax.random.randint(key_list[4], (HEADS,), 0, 8), jax.random.fold_in(key_list[4], 1), 0, 7).astype(jnp.int32),
        "head_gain": jnp.clip(1.0 + 0.18 * jax.random.normal(key_list[5], (HEADS, HD), jnp.float32), 0.1, 1.9),
    }


epsilon = 1e-06

def attend_head(bundle):
    query, key_item, value_item, state, gain_row = bundle
    factor = query.shape[1] ** (-0.5)
    scores = jnp.dot(query, key_item.T, preferred_element_type=jnp.float32) * factor
    row_top = lax.optimization_barrier(jnp.max(scores, axis=1, keepdims=True))
    weights = jnp.exp(scores - row_top)
    row_total = lax.optimization_barrier(jnp.sum(weights, axis=1, keepdims=True))
    numerator = jnp.dot(weights.astype(jnp.bfloat16), value_item, preferred_element_type=jnp.float32)
    carried = jnp.dot(query, state, preferred_element_type=jnp.float32) * factor
    mixed = numerator / row_total + carried
    normed = mixed * lax.rsqrt(lax.optimization_barrier(jnp.mean(mixed * mixed, axis=1, keepdims=True)) + epsilon) * gain_row
    return normed.astype(jnp.bfloat16)

def outer_sum(bundle):
    key_head, value_head = bundle
    return jnp.dot(key_head.T, value_head, preferred_element_type=jnp.float32)

def by_heads(block):
    return block.reshape(TOK_BLK, HEADS, HD).transpose(1, 0, 2)

def reference(queries, key_rows, value_rows, noise_level, decay_power, head_gain):
    powers = decay_power.astype(jnp.float32)
    levels = noise_level.astype(jnp.float32)
    rates = jnp.exp2(-(powers[None, :] * (0.25 + 1.75 * levels[:, None] / LEVELS)) / BLOCKS)

    def one_block(carried_state, inputs):
        query_block, key_block, value_block, rate_now = inputs
        query_heads = by_heads(query_block)
        key_heads = by_heads(key_block)
        value_heads = by_heads(value_block)
        fresh = lax.map(outer_sum, (key_heads, value_heads)) / TOK_BLK
        state = (rate_now[:, None, None] * carried_state).astype(jnp.bfloat16)
        outcome = lax.map(attend_head, (query_heads, key_heads, value_heads, state, head_gain))
        advanced = rate_now[:, None, None] * carried_state + fresh
        return (advanced, outcome.transpose(1, 0, 2).reshape(TOK_BLK, HEADS * HD))
    start = jnp.zeros((HEADS, HD, HD), jnp.float32)
    unused_state, attended = lax.scan(one_block, start, (queries, key_rows, value_rows, rates))
    return attended
```

```python
import functools

import jax
import jax.numpy as jnp
from jax import lax
from jax.experimental import pallas as pl
from jax.experimental.pallas import tpu as pltpu
from jax.sharding import PartitionSpec as P

LEVELS = 1000
HGROUPS = 8


epsilon = 1e-06


def carried_in(value, axis, join, neutral):
    count, mine = (lax.axis_size(axis), lax.axis_index(axis))
    pieces = jax.tree.map(lambda part: lax.all_gather(part, axis), value)
    so_far = jax.tree.map(
        lambda part, zero: jnp.full_like(part, 0) + jnp.asarray(zero, part.dtype), value, neutral
    )

    def lap(position, so_far):
        longer = join(so_far, jax.tree.map(lambda part: part[position], pieces))
        return jax.tree.map(lambda new, old: jnp.where(position < mine, new, old), longer, so_far)

    return lax.fori_loop(0, count - 1, lap, so_far)


def spread_items(block, quarters, heads_total, depth):
    part_rows = block.shape[0] // quarters
    shaped = block.reshape(quarters, part_rows, heads_total, depth).transpose(0, 2, 1, 3)
    return shaped.reshape(quarters * heads_total, part_rows, depth)


def copied_items(block, quarters, heads_total, depth):
    every = block.reshape(block.shape[0], heads_total, depth).transpose(1, 0, 2)
    copied = jnp.broadcast_to(every[None], (quarters,) + every.shape)
    return copied.reshape(quarters * heads_total, block.shape[0], depth)


def attend_head(bundle):
    query, key_item, value_item, state, gain_row = bundle
    factor = query.shape[1] ** (-0.5)
    scores = jnp.dot(query, key_item.T, preferred_element_type=jnp.float32) * factor
    row_top = jnp.max(scores, axis=1, keepdims=True)
    weights = jnp.exp(scores - row_top)
    row_total = jnp.sum(weights, axis=1, keepdims=True)
    numerator = jnp.dot(
        weights.astype(jnp.bfloat16), value_item, preferred_element_type=jnp.float32
    )
    carried = jnp.dot(query, state, preferred_element_type=jnp.float32) * factor
    mixed = numerator / row_total + carried
    normed = mixed * lax.rsqrt(jnp.mean(mixed * mixed, axis=1, keepdims=True) + epsilon) * gain_row
    return normed.astype(jnp.bfloat16)


def compose(earlier, later):
    return (earlier[0] * later[0], later[0][:, None, None] * earlier[1] + later[1])


MESH = pl.DeviceIdType.MESH


def partner(me, flips, count):
    other, digit = me, 1
    while digit < count:
        if flips & digit:
            other = other + digit * (1 - 2 * ((me // digit) % 2))
        digit *= 2
    return other


def fused_kernel(
    count, blocks, q_ref, k_ref, v_ref, noise_ref, power_ref, gain_ref, out_ref,
    q_all, k_all, v_all, outcome, fresh_mine, fresh_got,
    in_send, in_recv, out_send, out_recv, fresh_send, fresh_recv,
):
    rows = q_ref.shape[0]
    depth = gain_ref.shape[1]
    grouped = q_all.shape[0]
    total_rows = count * rows
    factor = depth ** (-0.5)
    me, now = lax.axis_index("space"), lax.axis_index("tm")
    peers = [partner(me, flips, count) for flips in range(count)]
    order = list(range(count // 2, count)) + list(range(count // 2 - 1, 0, -1))

    barrier = pltpu.get_barrier_semaphore()
    for flips in range(1, count):
        pl.semaphore_signal(barrier, inc=1, device_id={"space": peers[flips]}, device_id_type=MESH)
    for step in range(1, blocks):
        pl.semaphore_signal(
            barrier, inc=1, device_id={"tm": lax.rem(now + step, blocks)}, device_id_type=MESH
        )
    pl.semaphore_wait(barrier, count - 1 + blocks - 1)

    def lanes(head):
        return pl.ds(pl.multiple_of(head * depth, depth), depth)

    def part(device):
        return pl.ds(pl.multiple_of(device * rows, rows), rows)

    arrays = ((k_ref, k_all), (v_ref, v_all), (q_ref, q_all))
    for slot in range(grouped):
        for which, (source, target) in enumerate(arrays):
            for flips in order:
                pltpu.make_async_remote_copy(
                    src_ref=source.at[:, lanes(peers[flips] * grouped + slot)],
                    dst_ref=target.at[slot, part(me)],
                    send_sem=in_send.at[slot, which],
                    recv_sem=in_recv.at[slot, which],
                    device_id={"space": peers[flips]},
                    device_id_type=MESH,
                ).start()
            pltpu.make_async_copy(
                source.at[:, lanes(me * grouped + slot)],
                target.at[slot, part(me)],
                in_recv.at[slot, which],
            ).start()

    def arrived(slot, which):
        whole = arrays[which][1].at[slot]
        pltpu.make_async_copy(whole, whole, in_recv.at[slot, which]).wait()

    level = jnp.full((8, depth), noise_ref[0], jnp.int32).astype(jnp.float32)
    for slot in range(grouped):
        head = me * grouped + slot
        power = jnp.full((8, depth), power_ref[head], jnp.int32).astype(jnp.float32)
        rate = jnp.exp2(-(power * (0.25 + 1.75 * level / LEVELS)) / blocks)
        arrived(slot, 0)
        arrived(slot, 1)
        fresh = lax.dot_general(
            k_all[slot], v_all[slot], (((0,), (0,)), ((), ())), preferred_element_type=jnp.float32
        )
        fresh_mine[slot, 0:depth, :] = fresh / total_rows
        fresh_mine[slot, depth : depth + 8, :] = rate
        for step in range(1, blocks):
            pltpu.make_async_remote_copy(
                src_ref=fresh_mine.at[slot],
                dst_ref=fresh_got.at[slot, step - 1],
                send_sem=fresh_send.at[slot],
                recv_sem=fresh_recv.at[slot],
                device_id={"tm": lax.rem(now + step, blocks)},
                device_id_type=MESH,
            ).start()
        arrived(slot, 2)
        landed = fresh_got.at[slot]
        pltpu.make_async_copy(landed, landed, fresh_recv.at[slot]).wait()
        carried = jnp.zeros((depth, depth), jnp.float32)
        for step in range(blocks - 1, 0, -1):
            longer = (
                fresh_got[slot, step - 1, depth : depth + 1, :] * carried
                + fresh_got[slot, step - 1, 0:depth, :]
            )
            carried = jnp.where(now - step >= 0, longer, carried)
        state = (rate[0:1, :] * carried).astype(jnp.bfloat16)
        gain_row = gain_ref[pl.ds(head, 1), :]

        def attend(device):
            query = q_all[slot, part(device), :]
            scores = lax.dot_general(
                query, k_all[slot], (((1,), (1,)), ((), ())), preferred_element_type=jnp.float32
            ) * factor
            weights = jnp.exp(scores - jnp.max(scores, axis=1, keepdims=True))
            row_total = jnp.sum(weights, axis=1, keepdims=True)
            numerator = jnp.dot(
                weights.astype(jnp.bfloat16), v_all[slot], preferred_element_type=jnp.float32
            )
            before = jnp.dot(query, state, preferred_element_type=jnp.float32) * factor
            mixed = numerator / row_total + before
            scale = lax.rsqrt(jnp.mean(mixed * mixed, axis=1, keepdims=True) + epsilon)
            outcome[slot, part(device), :] = (mixed * scale * gain_row).astype(jnp.bfloat16)

        for flips in order:
            attend(peers[flips])
            pltpu.make_async_remote_copy(
                src_ref=outcome.at[slot, part(peers[flips])],
                dst_ref=out_ref.at[:, lanes(head)],
                send_sem=out_send.at[slot],
                recv_sem=out_recv.at[0],
                device_id={"space": peers[flips]},
                device_id_type=MESH,
            ).start()
        attend(me)
        pltpu.make_async_copy(
            outcome.at[slot, part(me)], out_ref.at[:, lanes(head)], out_recv.at[0]
        ).start()

    for slot in range(grouped):
        for which in range(len(arrays)):
            sent = arrays[which][1].at[slot, pl.ds(0, total_rows - rows)]
            pltpu.make_async_copy(sent, sent, in_send.at[slot, which]).wait()
        landed = fresh_got.at[slot]
        pltpu.make_async_copy(landed, landed, fresh_send.at[slot]).wait()
        returned = outcome.at[slot, pl.ds(0, total_rows - rows)]
        pltpu.make_async_copy(returned, returned, out_send.at[slot]).wait()
    pltpu.make_async_copy(out_ref, out_ref, out_recv.at[0]).wait()


def fused(queries, key_rows, value_rows, noise_level, decay_power, head_gain):
    count, blocks = lax.axis_size("space"), lax.axis_size("tm")
    rows, width = queries.shape[1:]
    heads_total, depth = head_gain.shape
    grouped = heads_total // count
    gathered = pltpu.VMEM((grouped, count * rows, depth), jnp.bfloat16)
    dma = pltpu.SemaphoreType.DMA
    out = pl.pallas_call(
        functools.partial(fused_kernel, count, blocks),
        out_shape=jax.ShapeDtypeStruct((rows, width), jnp.bfloat16),
        in_specs=[pl.BlockSpec(memory_space=pl.ANY)] * 3
        + [pl.BlockSpec(memory_space=pltpu.SMEM)] * 2
        + [pl.BlockSpec(memory_space=pltpu.VMEM)],
        out_specs=pl.BlockSpec(memory_space=pl.ANY),
        scratch_shapes=[
            gathered,
            gathered,
            gathered,
            gathered,
            pltpu.VMEM((grouped, depth + 8, depth), jnp.float32),
            pltpu.VMEM((grouped, blocks - 1, depth + 8, depth), jnp.float32),
            dma((grouped, 3)),
            dma((grouped, 3)),
            dma((grouped,)),
            dma((1,)),
            dma((grouped,)),
            dma((grouped,)),
        ],
        compiler_params=pltpu.CompilerParams(collective_id=0, has_side_effects=True),
        name="heads_exchange",
    )(queries[0], key_rows[0], value_rows[0], noise_level, decay_power, head_gain)
    return out[None]


def body(queries, key_rows, value_rows, noise_level, decay_power, head_gain):
    heads_total = decay_power.shape[0]
    depth = head_gain.shape[1]
    local_rows = queries.shape[1]
    quarters = lax.axis_size("space") // HGROUPS
    grouped = heads_total // HGROUPS
    query_items = spread_items(queries[0], quarters, heads_total, depth)
    keys_sent = copied_items(key_rows[0], quarters, heads_total, depth)
    values_sent = copied_items(value_rows[0], quarters, heads_total, depth)
    query_got, keys_got, values_got = (
        lax.all_to_all(query_items, "space", split_axis=0, concat_axis=1, tiled=True),
        lax.all_to_all(keys_sent, "space", split_axis=0, concat_axis=1, tiled=True),
        lax.all_to_all(values_sent, "space", split_axis=0, concat_axis=1, tiled=True),
    )
    key_count = keys_got.shape[1]
    fresh = (
        jnp.einsum("inh,ine->ihe", keys_got, values_got, preferred_element_type=jnp.float32)
        / key_count
    )
    group_index = lax.axis_index("space") % HGROUPS
    powers = lax.dynamic_slice_in_dim(decay_power, group_index * grouped, grouped).astype(
        jnp.float32
    )
    level_now = noise_level[0].astype(jnp.float32)
    block_count = lax.axis_size("tm")
    rate = jnp.exp2(-(powers * (0.25 + 1.75 * level_now / LEVELS)) / block_count)
    zeros_state = jnp.zeros_like(fresh)
    unused_rate, before = carried_in(
        (rate, fresh), "tm", compose, (jnp.ones_like(rate), zeros_state)
    )
    state = (rate[:, None, None] * before).astype(jnp.bfloat16)
    gain_rows = lax.dynamic_slice_in_dim(head_gain, group_index * grouped, grouped)
    outcome = lax.map(attend_head, (query_got, keys_got, values_got, state, gain_rows))
    returned = lax.all_to_all(outcome, "space", split_axis=1, concat_axis=0, tiled=True)
    part_rows = local_rows // quarters
    restored = returned.reshape(quarters, heads_total, part_rows, depth).transpose(0, 2, 1, 3)
    return restored.reshape(1, local_rows, heads_total * depth)


def solution(mesh):
    in_specs = (
        P("tm", "space", None),
        P("tm", "space", None),
        P("tm", "space", None),
        P("tm"),
        P(),
        P(),
    )
    out_specs = P("tm", "space", None)
    step = fused if mesh.shape["space"] == HGROUPS else body
    return jax.shard_map(step, mesh=mesh, in_specs=in_specs, out_specs=out_specs, check_vma=False)
```

```python
import functools

import jax
import jax.numpy as jnp
from jax import lax
from jax.experimental import pallas as pl
from jax.experimental.pallas import tpu as pltpu
from jax.sharding import PartitionSpec as P

LEVELS = 1000
HGROUPS = 8
VMEM_GRANT = 32 * 2**20


epsilon = 1e-06


def carried_in(value, axis, join, neutral):
    count, mine = (lax.axis_size(axis), lax.axis_index(axis))
    pieces = jax.tree.map(lambda part: lax.all_gather(part, axis), value)
    so_far = jax.tree.map(
        lambda part, zero: jnp.full_like(part, 0) + jnp.asarray(zero, part.dtype), value, neutral
    )

    def lap(position, so_far):
        longer = join(so_far, jax.tree.map(lambda part: part[position], pieces))
        return jax.tree.map(lambda new, old: jnp.where(position < mine, new, old), longer, so_far)

    return lax.fori_loop(0, count - 1, lap, so_far)


def spread_items(block, quarters, heads_total, depth):
    part_rows = block.shape[0] // quarters
    shaped = block.reshape(quarters, part_rows, heads_total, depth).transpose(0, 2, 1, 3)
    return shaped.reshape(quarters * heads_total, part_rows, depth)


def copied_items(block, quarters, heads_total, depth):
    every = block.reshape(block.shape[0], heads_total, depth).transpose(1, 0, 2)
    copied = jnp.broadcast_to(every[None], (quarters,) + every.shape)
    return copied.reshape(quarters * heads_total, block.shape[0], depth)


def attend_head(bundle):
    query, key_item, value_item, state, gain_row = bundle
    factor = query.shape[1] ** (-0.5)
    scores = jnp.dot(query, key_item.T, preferred_element_type=jnp.float32) * factor
    row_top = jnp.max(scores, axis=1, keepdims=True)
    weights = jnp.exp(scores - row_top)
    row_total = jnp.sum(weights, axis=1, keepdims=True)
    numerator = jnp.dot(
        weights.astype(jnp.bfloat16), value_item, preferred_element_type=jnp.float32
    )
    carried = jnp.dot(query, state, preferred_element_type=jnp.float32) * factor
    mixed = numerator / row_total + carried
    normed = mixed * lax.rsqrt(jnp.mean(mixed * mixed, axis=1, keepdims=True) + epsilon) * gain_row
    return normed.astype(jnp.bfloat16)


def compose(earlier, later):
    return (earlier[0] * later[0], later[0][:, None, None] * earlier[1] + later[1])


MESH = pl.DeviceIdType.MESH


def partner(me, flips, count):
    other, digit = me, 1
    while digit < count:
        if flips & digit:
            other = other + digit * (1 - 2 * ((me // digit) % 2))
        digit *= 2
    return other


def fused_kernel(
    count, blocks, q_ref, k_ref, v_ref, noise_ref, power_hbm, gain_hbm, out_ref,
    power_ref, gain_ref, small_done,
    q_all, k_all, v_all, outcome, fresh_mine, fresh_got,
    in_send, in_recv, out_send, out_recv, fresh_send, fresh_recv,
):
    rows = q_ref.shape[0]
    depth = gain_ref.shape[1]
    grouped = q_all.shape[0]
    total_rows = count * rows
    factor = depth ** (-0.5)
    me, now = lax.axis_index("space"), lax.axis_index("tm")
    peers = [partner(me, flips, count) for flips in range(count)]
    order = list(range(1, count))

    small = [
        pltpu.make_async_copy(held, here, small_done.at[index])
        for index, (held, here) in enumerate(
            ((power_hbm, power_ref), (gain_hbm, gain_ref))
        )
    ]
    for copy in small:
        copy.start()

    barrier = pltpu.get_barrier_semaphore()
    for flips in range(1, count):
        pl.semaphore_signal(barrier, inc=1, device_id={"space": peers[flips]}, device_id_type=MESH)
    for step in range(1, blocks):
        pl.semaphore_signal(
            barrier, inc=1, device_id={"tm": lax.rem(now + step, blocks)}, device_id_type=MESH
        )
    pl.semaphore_wait(barrier, count - 1 + blocks - 1)

    def lanes(head):
        return pl.ds(pl.multiple_of(head * depth, depth), depth)

    def part(device):
        return pl.ds(pl.multiple_of(device * rows, rows), rows)

    arrays = ((k_ref, k_all), (v_ref, v_all), (q_ref, q_all))
    def send_inputs(slot, others):
        for which, (source, target) in enumerate(arrays):
            for flips in others:
                pltpu.make_async_remote_copy(
                    src_ref=source.at[:, lanes(peers[flips] * grouped + slot)],
                    dst_ref=target.at[slot, part(me)],
                    send_sem=in_send.at[slot, which],
                    recv_sem=in_recv.at[slot, which],
                    device_id={"space": peers[flips]},
                    device_id_type=MESH,
                ).start()

    near, far = order[: count // 2 - 1], order[count // 2 - 1 :]
    for slot in range(grouped):
        send_inputs(slot, near)
    for slot in range(grouped):
        send_inputs(slot, far)
    for slot in range(grouped):
        for which, (source, target) in enumerate(arrays):
            pltpu.make_async_copy(
                source.at[:, lanes(me * grouped + slot)],
                target.at[slot, part(me)],
                in_recv.at[slot, which],
            ).start()

    def arrived(slot, which):
        whole = arrays[which][1].at[slot]
        pltpu.make_async_copy(whole, whole, in_recv.at[slot, which]).wait()

    def give_back(slot, flips):
        pltpu.make_async_remote_copy(
            src_ref=outcome.at[slot, part(peers[flips])],
            dst_ref=out_ref.at[:, lanes(me * grouped + slot)],
            send_sem=out_send.at[slot],
            recv_sem=out_recv.at[0],
            device_id={"space": peers[flips]},
            device_id_type=MESH,
        ).start()

    for copy in small:
        copy.wait()
    level = jnp.full((8, depth), noise_ref[0], jnp.int32).astype(jnp.float32)
    for slot in range(grouped):
        head = me * grouped + slot
        power = jnp.full((8, depth), power_ref[head], jnp.int32).astype(jnp.float32)
        rate = jnp.exp2(-(power * (0.25 + 1.75 * level / LEVELS)) / blocks)
        arrived(slot, 0)
        if slot == grouped - 1:
            for earlier in range(slot):
                for flips in order:
                    give_back(earlier, flips)
        arrived(slot, 1)
        fresh = lax.dot_general(
            k_all[slot], v_all[slot], (((0,), (0,)), ((), ())), preferred_element_type=jnp.float32
        )
        fresh_mine[slot, 0:depth, :] = fresh / total_rows
        fresh_mine[slot, depth : depth + 8, :] = rate
        for step in range(1, blocks):
            pltpu.make_async_remote_copy(
                src_ref=fresh_mine.at[slot],
                dst_ref=fresh_got.at[slot, step - 1],
                send_sem=fresh_send.at[slot],
                recv_sem=fresh_recv.at[slot],
                device_id={"tm": lax.rem(now + step, blocks)},
                device_id_type=MESH,
            ).start()
        arrived(slot, 2)
        landed = fresh_got.at[slot]
        pltpu.make_async_copy(landed, landed, fresh_recv.at[slot]).wait()
        carried = jnp.zeros((depth, depth), jnp.float32)
        for step in range(blocks - 1, 0, -1):
            longer = (
                fresh_got[slot, step - 1, depth : depth + 1, :] * carried
                + fresh_got[slot, step - 1, 0:depth, :]
            )
            carried = jnp.where(now - step >= 0, longer, carried)
        state = (rate[0:1, :] * carried).astype(jnp.bfloat16)
        gain_row = gain_ref[pl.ds(head, 1), :]

        def attend(device):
            query = q_all[slot, part(device), :]
            scores = lax.dot_general(
                query, k_all[slot], (((1,), (1,)), ((), ())), preferred_element_type=jnp.float32
            ) * factor
            weights = jnp.exp(scores - jnp.max(scores, axis=1, keepdims=True))
            row_total = jnp.sum(weights, axis=1, keepdims=True)
            numerator = jnp.dot(
                weights.astype(jnp.bfloat16), v_all[slot], preferred_element_type=jnp.float32
            )
            before = jnp.dot(query, state, preferred_element_type=jnp.float32) * factor
            mixed = numerator / row_total + before
            scale = lax.rsqrt(jnp.mean(mixed * mixed, axis=1, keepdims=True) + epsilon)
            outcome[slot, part(device), :] = (mixed * scale * gain_row).astype(jnp.bfloat16)

        for flips in order:
            attend(peers[flips])
            if slot == grouped - 1:
                give_back(slot, flips)
        attend(me)
        pltpu.make_async_copy(
            outcome.at[slot, part(me)], out_ref.at[:, lanes(head)], out_recv.at[0]
        ).start()

    for slot in range(grouped):
        for which in range(len(arrays)):
            sent = arrays[which][1].at[slot, pl.ds(0, total_rows - rows)]
            pltpu.make_async_copy(sent, sent, in_send.at[slot, which]).wait()
        landed = fresh_got.at[slot]
        pltpu.make_async_copy(landed, landed, fresh_send.at[slot]).wait()
        returned = outcome.at[slot, pl.ds(0, total_rows - rows)]
        pltpu.make_async_copy(returned, returned, out_send.at[slot]).wait()
    pltpu.make_async_copy(out_ref, out_ref, out_recv.at[0]).wait()


def fused(queries, key_rows, value_rows, noise_level, decay_power, head_gain):
    count, blocks = lax.axis_size("space"), lax.axis_size("tm")
    rows, width = queries.shape[1:]
    heads_total, depth = head_gain.shape
    grouped = heads_total // count
    held = [
        pltpu.with_memory_space_constraint(operand, pltpu.HBM)
        for operand in (queries[0], key_rows[0], value_rows[0], decay_power, head_gain)
    ]
    gathered = pltpu.VMEM((grouped, count * rows, depth), jnp.bfloat16)
    dma = pltpu.SemaphoreType.DMA
    out = pl.pallas_call(
        functools.partial(fused_kernel, count, blocks),
        out_shape=jax.ShapeDtypeStruct((rows, width), jnp.bfloat16),
        in_specs=[pl.BlockSpec(memory_space=pl.ANY)] * 3
        + [pl.BlockSpec(memory_space=pltpu.SMEM)]
        + [pl.BlockSpec(memory_space=pl.ANY)] * 2,
        out_specs=pl.BlockSpec(memory_space=pl.ANY),
        scratch_shapes=[
            pltpu.SMEM(decay_power.shape, jnp.int32),
            pltpu.VMEM(head_gain.shape, jnp.float32),
            dma((2,)),
            gathered,
            gathered,
            gathered,
            gathered,
            pltpu.VMEM((grouped, depth + 8, depth), jnp.float32),
            pltpu.VMEM((grouped, blocks - 1, depth + 8, depth), jnp.float32),
            dma((grouped, 3)),
            dma((grouped, 3)),
            dma((grouped,)),
            dma((1,)),
            dma((grouped,)),
            dma((grouped,)),
        ],
        compiler_params=pltpu.CompilerParams(collective_id=0, has_side_effects=True, vmem_limit_bytes=VMEM_GRANT),
        name="heads_exchange",
    )(*held[:3], noise_level, *held[3:])
    return out[None]


def body(queries, key_rows, value_rows, noise_level, decay_power, head_gain):
    heads_total = decay_power.shape[0]
    depth = head_gain.shape[1]
    local_rows = queries.shape[1]
    quarters = lax.axis_size("space") // HGROUPS
    grouped = heads_total // HGROUPS
    query_items = spread_items(queries[0], quarters, heads_total, depth)
    keys_sent = copied_items(key_rows[0], quarters, heads_total, depth)
    values_sent = copied_items(value_rows[0], quarters, heads_total, depth)
    query_got, keys_got, values_got = (
        lax.all_to_all(query_items, "space", split_axis=0, concat_axis=1, tiled=True),
        lax.all_to_all(keys_sent, "space", split_axis=0, concat_axis=1, tiled=True),
        lax.all_to_all(values_sent, "space", split_axis=0, concat_axis=1, tiled=True),
    )
    key_count = keys_got.shape[1]
    fresh = (
        jnp.einsum("inh,ine->ihe", keys_got, values_got, preferred_element_type=jnp.float32)
        / key_count
    )
    group_index = lax.axis_index("space") % HGROUPS
    powers = lax.dynamic_slice_in_dim(decay_power, group_index * grouped, grouped).astype(
        jnp.float32
    )
    level_now = noise_level[0].astype(jnp.float32)
    block_count = lax.axis_size("tm")
    rate = jnp.exp2(-(powers * (0.25 + 1.75 * level_now / LEVELS)) / block_count)
    zeros_state = jnp.zeros_like(fresh)
    unused_rate, before = carried_in(
        (rate, fresh), "tm", compose, (jnp.ones_like(rate), zeros_state)
    )
    state = (rate[:, None, None] * before).astype(jnp.bfloat16)
    gain_rows = lax.dynamic_slice_in_dim(head_gain, group_index * grouped, grouped)
    outcome = lax.map(attend_head, (query_got, keys_got, values_got, state, gain_rows))
    returned = lax.all_to_all(outcome, "space", split_axis=1, concat_axis=0, tiled=True)
    part_rows = local_rows // quarters
    restored = returned.reshape(quarters, heads_total, part_rows, depth).transpose(0, 2, 1, 3)
    return restored.reshape(1, local_rows, heads_total * depth)


def solution(mesh):
    in_specs = (
        P("tm", "space", None),
        P("tm", "space", None),
        P("tm", "space", None),
        P("tm"),
        P(),
        P(),
    )
    out_specs = P("tm", "space", None)
    step = fused if mesh.shape["space"] == HGROUPS else body
    return jax.shard_map(step, mesh=mesh, in_specs=in_specs, out_specs=out_specs, check_vma=False)
```

```python
import functools

import jax
import jax.numpy as jnp
from jax import lax
from jax.experimental import pallas as pl
from jax.experimental.pallas import tpu as pltpu
from jax.sharding import PartitionSpec as P

LEVELS = 1000
HGROUPS = 8
VMEM_GRANT = 32 * 2**20


epsilon = 1e-06


def carried_in(value, axis, join, neutral):
    count, mine = (lax.axis_size(axis), lax.axis_index(axis))
    pieces = jax.tree.map(lambda part: lax.all_gather(part, axis), value)
    so_far = jax.tree.map(
        lambda part, zero: jnp.full_like(part, 0) + jnp.asarray(zero, part.dtype), value, neutral
    )

    def lap(position, so_far):
        longer = join(so_far, jax.tree.map(lambda part: part[position], pieces))
        return jax.tree.map(lambda new, old: jnp.where(position < mine, new, old), longer, so_far)

    return lax.fori_loop(0, count - 1, lap, so_far)


def spread_items(block, quarters, heads_total, depth):
    part_rows = block.shape[0] // quarters
    shaped = block.reshape(quarters, part_rows, heads_total, depth).transpose(0, 2, 1, 3)
    return shaped.reshape(quarters * heads_total, part_rows, depth)


def copied_items(block, quarters, heads_total, depth):
    every = block.reshape(block.shape[0], heads_total, depth).transpose(1, 0, 2)
    copied = jnp.broadcast_to(every[None], (quarters,) + every.shape)
    return copied.reshape(quarters * heads_total, block.shape[0], depth)


def attend_head(bundle):
    query, key_item, value_item, state, gain_row = bundle
    factor = query.shape[1] ** (-0.5)
    scores = jnp.dot(query, key_item.T, preferred_element_type=jnp.float32) * factor
    row_top = jnp.max(scores, axis=1, keepdims=True)
    weights = jnp.exp(scores - row_top)
    row_total = jnp.sum(weights, axis=1, keepdims=True)
    numerator = jnp.dot(
        weights.astype(jnp.bfloat16), value_item, preferred_element_type=jnp.float32
    )
    carried = jnp.dot(query, state, preferred_element_type=jnp.float32) * factor
    mixed = numerator / row_total + carried
    normed = mixed * lax.rsqrt(jnp.mean(mixed * mixed, axis=1, keepdims=True) + epsilon) * gain_row
    return normed.astype(jnp.bfloat16)


def compose(earlier, later):
    return (earlier[0] * later[0], later[0][:, None, None] * earlier[1] + later[1])


MESH = pl.DeviceIdType.MESH


def partner(me, flips, count):
    other, digit = me, 1
    while digit < count:
        if flips & digit:
            other = other + digit * (1 - 2 * ((me // digit) % 2))
        digit *= 2
    return other


def fused_kernel(
    count, blocks, q_ref, k_ref, v_ref, noise_ref, power_hbm, gain_hbm, out_ref,
    power_ref, gain_ref, small_done,
    q_all, k_all, v_all, outcome, fresh_mine, fresh_got,
    in_send, in_recv, out_send, out_recv, fresh_send, fresh_recv,
):
    rows = q_ref.shape[0]
    depth = gain_ref.shape[1]
    grouped = q_all.shape[0]
    total_rows = count * rows
    factor = depth ** (-0.5)
    me, now = lax.axis_index("space"), lax.axis_index("tm")
    peers = [partner(me, flips, count) for flips in range(count)]
    order = list(range(1, count))

    small = [
        pltpu.make_async_copy(held, here, small_done.at[index])
        for index, (held, here) in enumerate(
            ((power_hbm, power_ref), (gain_hbm, gain_ref))
        )
    ]
    for copy in small:
        copy.start()

    barrier = pltpu.get_barrier_semaphore()
    for flips in range(1, count):
        pl.semaphore_signal(barrier, inc=1, device_id={"space": peers[flips]}, device_id_type=MESH)
    for step in range(1, blocks):
        pl.semaphore_signal(
            barrier, inc=1, device_id={"tm": lax.rem(now + step, blocks)}, device_id_type=MESH
        )
    pl.semaphore_wait(barrier, count - 1 + blocks - 1)

    def lanes(head):
        return pl.ds(pl.multiple_of(head * depth, depth), depth)

    def part(device):
        return pl.ds(pl.multiple_of(device * rows, rows), rows)

    arrays = ((k_ref, k_all), (v_ref, v_all), (q_ref, q_all))
    def send_inputs(slot, others):
        for which, (source, target) in enumerate(arrays):
            for flips in others:
                pltpu.make_async_remote_copy(
                    src_ref=source.at[:, lanes(peers[flips] * grouped + slot)],
                    dst_ref=target.at[slot, part(me)],
                    send_sem=in_send.at[slot, which],
                    recv_sem=in_recv.at[slot, which],
                    device_id={"space": peers[flips]},
                    device_id_type=MESH,
                ).start()

    near, far = order[: count // 2 - 1], order[count // 2 - 1 :]
    for slot in range(grouped):
        send_inputs(slot, near)
    for slot in range(grouped):
        send_inputs(slot, far)
    for slot in range(grouped):
        for which, (source, target) in enumerate(arrays):
            pltpu.make_async_copy(
                source.at[:, lanes(me * grouped + slot)],
                target.at[slot, part(me)],
                in_recv.at[slot, which],
            ).start()

    def arrived(slot, which):
        whole = arrays[which][1].at[slot]
        pltpu.make_async_copy(whole, whole, in_recv.at[slot, which]).wait()

    def give_back(slot, flips):
        pltpu.make_async_remote_copy(
            src_ref=outcome.at[slot, part(peers[flips])],
            dst_ref=out_ref.at[:, lanes(me * grouped + slot)],
            send_sem=out_send.at[slot],
            recv_sem=out_recv.at[0],
            device_id={"space": peers[flips]},
            device_id_type=MESH,
        ).start()

    for copy in small:
        copy.wait()
    level = jnp.full((8, depth), noise_ref[0], jnp.int32).astype(jnp.float32)
    for slot in range(grouped):
        head = me * grouped + slot
        power = jnp.full((8, depth), power_ref[head], jnp.int32).astype(jnp.float32)
        rate = jnp.exp2(-(power * (0.25 + 1.75 * level / LEVELS)) / blocks)
        arrived(slot, 0)
        arrived(slot, 1)
        fresh = lax.dot_general(
            k_all[slot], v_all[slot], (((0,), (0,)), ((), ())), preferred_element_type=jnp.float32
        )
        fresh_mine[slot, 0:depth, :] = fresh / total_rows
        fresh_mine[slot, depth : depth + 8, :] = rate
        for step in range(1, blocks):
            pltpu.make_async_remote_copy(
                src_ref=fresh_mine.at[slot],
                dst_ref=fresh_got.at[slot, step - 1],
                send_sem=fresh_send.at[slot],
                recv_sem=fresh_recv.at[slot],
                device_id={"tm": lax.rem(now + step, blocks)},
                device_id_type=MESH,
            ).start()
        arrived(slot, 2)
        landed = fresh_got.at[slot]
        pltpu.make_async_copy(landed, landed, fresh_recv.at[slot]).wait()
        carried = jnp.zeros((depth, depth), jnp.float32)
        for step in range(blocks - 1, 0, -1):
            longer = (
                fresh_got[slot, step - 1, depth : depth + 1, :] * carried
                + fresh_got[slot, step - 1, 0:depth, :]
            )
            carried = jnp.where(now - step >= 0, longer, carried)
        state = (rate[0:1, :] * carried).astype(jnp.bfloat16)
        gain_row = gain_ref[pl.ds(head, 1), :]

        def attend(device):
            query = q_all[slot, part(device), :]
            scores = lax.dot_general(
                query, k_all[slot], (((1,), (1,)), ((), ())), preferred_element_type=jnp.float32
            ) * factor
            weights = jnp.exp(scores - jnp.max(scores, axis=1, keepdims=True))
            row_total = jnp.sum(weights, axis=1, keepdims=True)
            numerator = jnp.dot(
                weights.astype(jnp.bfloat16), v_all[slot], preferred_element_type=jnp.float32
            )
            before = jnp.dot(query, state, preferred_element_type=jnp.float32) * factor
            mixed = numerator / row_total + before
            scale = lax.rsqrt(jnp.mean(mixed * mixed, axis=1, keepdims=True) + epsilon)
            outcome[slot, part(device), :] = (mixed * scale * gain_row).astype(jnp.bfloat16)

        for flips in order:
            attend(peers[flips])
            if slot == grouped - 1:
                give_back(slot, flips)
        attend(me)
        if slot == grouped - 2:
            for earlier in range(slot + 1):
                for flips in far + near:
                    give_back(earlier, flips)
        pltpu.make_async_copy(
            outcome.at[slot, part(me)], out_ref.at[:, lanes(head)], out_recv.at[0]
        ).start()

    for slot in range(grouped):
        for which in range(len(arrays)):
            sent = arrays[which][1].at[slot, pl.ds(0, total_rows - rows)]
            pltpu.make_async_copy(sent, sent, in_send.at[slot, which]).wait()
        landed = fresh_got.at[slot]
        pltpu.make_async_copy(landed, landed, fresh_send.at[slot]).wait()
        returned = outcome.at[slot, pl.ds(0, total_rows - rows)]
        pltpu.make_async_copy(returned, returned, out_send.at[slot]).wait()
    pltpu.make_async_copy(out_ref, out_ref, out_recv.at[0]).wait()


def fused(queries, key_rows, value_rows, noise_level, decay_power, head_gain):
    count, blocks = lax.axis_size("space"), lax.axis_size("tm")
    rows, width = queries.shape[1:]
    heads_total, depth = head_gain.shape
    grouped = heads_total // count
    held = [
        pltpu.with_memory_space_constraint(operand, pltpu.HBM)
        for operand in (queries[0], key_rows[0], value_rows[0], decay_power, head_gain)
    ]
    gathered = pltpu.VMEM((grouped, count * rows, depth), jnp.bfloat16)
    dma = pltpu.SemaphoreType.DMA
    out = pl.pallas_call(
        functools.partial(fused_kernel, count, blocks),
        out_shape=jax.ShapeDtypeStruct((rows, width), jnp.bfloat16),
        in_specs=[pl.BlockSpec(memory_space=pl.ANY)] * 3
        + [pl.BlockSpec(memory_space=pltpu.SMEM)]
        + [pl.BlockSpec(memory_space=pl.ANY)] * 2,
        out_specs=pl.BlockSpec(memory_space=pl.ANY),
        scratch_shapes=[
            pltpu.SMEM(decay_power.shape, jnp.int32),
            pltpu.VMEM(head_gain.shape, jnp.float32),
            dma((2,)),
            gathered,
            gathered,
            gathered,
            gathered,
            pltpu.VMEM((grouped, depth + 8, depth), jnp.float32),
            pltpu.VMEM((grouped, blocks - 1, depth + 8, depth), jnp.float32),
            dma((grouped, 3)),
            dma((grouped, 3)),
            dma((grouped,)),
            dma((1,)),
            dma((grouped,)),
            dma((grouped,)),
        ],
        compiler_params=pltpu.CompilerParams(collective_id=0, has_side_effects=True, vmem_limit_bytes=VMEM_GRANT),
        name="heads_exchange",
    )(*held[:3], noise_level, *held[3:])
    return out[None]


def body(queries, key_rows, value_rows, noise_level, decay_power, head_gain):
    heads_total = decay_power.shape[0]
    depth = head_gain.shape[1]
    local_rows = queries.shape[1]
    quarters = lax.axis_size("space") // HGROUPS
    grouped = heads_total // HGROUPS
    query_items = spread_items(queries[0], quarters, heads_total, depth)
    keys_sent = copied_items(key_rows[0], quarters, heads_total, depth)
    values_sent = copied_items(value_rows[0], quarters, heads_total, depth)
    query_got, keys_got, values_got = (
        lax.all_to_all(query_items, "space", split_axis=0, concat_axis=1, tiled=True),
        lax.all_to_all(keys_sent, "space", split_axis=0, concat_axis=1, tiled=True),
        lax.all_to_all(values_sent, "space", split_axis=0, concat_axis=1, tiled=True),
    )
    key_count = keys_got.shape[1]
    fresh = (
        jnp.einsum("inh,ine->ihe", keys_got, values_got, preferred_element_type=jnp.float32)
        / key_count
    )
    group_index = lax.axis_index("space") % HGROUPS
    powers = lax.dynamic_slice_in_dim(decay_power, group_index * grouped, grouped).astype(
        jnp.float32
    )
    level_now = noise_level[0].astype(jnp.float32)
    block_count = lax.axis_size("tm")
    rate = jnp.exp2(-(powers * (0.25 + 1.75 * level_now / LEVELS)) / block_count)
    zeros_state = jnp.zeros_like(fresh)
    unused_rate, before = carried_in(
        (rate, fresh), "tm", compose, (jnp.ones_like(rate), zeros_state)
    )
    state = (rate[:, None, None] * before).astype(jnp.bfloat16)
    gain_rows = lax.dynamic_slice_in_dim(head_gain, group_index * grouped, grouped)
    outcome = lax.map(attend_head, (query_got, keys_got, values_got, state, gain_rows))
    returned = lax.all_to_all(outcome, "space", split_axis=1, concat_axis=0, tiled=True)
    part_rows = local_rows // quarters
    restored = returned.reshape(quarters, heads_total, part_rows, depth).transpose(0, 2, 1, 3)
    return restored.reshape(1, local_rows, heads_total * depth)


def solution(mesh):
    in_specs = (
        P("tm", "space", None),
        P("tm", "space", None),
        P("tm", "space", None),
        P("tm"),
        P(),
        P(),
    )
    out_specs = P("tm", "space", None)
    step = fused if mesh.shape["space"] == HGROUPS else body
    return jax.shard_map(step, mesh=mesh, in_specs=in_specs, out_specs=out_specs, check_vma=False)
```

```python
import functools

import jax
import jax.numpy as jnp
from jax import lax
from jax.experimental import pallas as pl
from jax.experimental.pallas import tpu as pltpu
from jax.sharding import PartitionSpec as P

LEVELS = 1000
HGROUPS = 8
VMEM_GRANT = 32 * 2**20


epsilon = 1e-06


def carried_in(value, axis, join, neutral):
    count, mine = (lax.axis_size(axis), lax.axis_index(axis))
    pieces = jax.tree.map(lambda part: lax.all_gather(part, axis), value)
    so_far = jax.tree.map(
        lambda part, zero: jnp.full_like(part, 0) + jnp.asarray(zero, part.dtype), value, neutral
    )

    def lap(position, so_far):
        longer = join(so_far, jax.tree.map(lambda part: part[position], pieces))
        return jax.tree.map(lambda new, old: jnp.where(position < mine, new, old), longer, so_far)

    return lax.fori_loop(0, count - 1, lap, so_far)


def spread_items(block, quarters, heads_total, depth):
    part_rows = block.shape[0] // quarters
    shaped = block.reshape(quarters, part_rows, heads_total, depth).transpose(0, 2, 1, 3)
    return shaped.reshape(quarters * heads_total, part_rows, depth)


def copied_items(block, quarters, heads_total, depth):
    every = block.reshape(block.shape[0], heads_total, depth).transpose(1, 0, 2)
    copied = jnp.broadcast_to(every[None], (quarters,) + every.shape)
    return copied.reshape(quarters * heads_total, block.shape[0], depth)


def attend_head(bundle):
    query, key_item, value_item, state, gain_row = bundle
    factor = query.shape[1] ** (-0.5)
    scores = jnp.dot(query, key_item.T, preferred_element_type=jnp.float32) * factor
    row_top = jnp.max(scores, axis=1, keepdims=True)
    weights = jnp.exp(scores - row_top)
    row_total = jnp.sum(weights, axis=1, keepdims=True)
    numerator = jnp.dot(
        weights.astype(jnp.bfloat16), value_item, preferred_element_type=jnp.float32
    )
    carried = jnp.dot(query, state, preferred_element_type=jnp.float32) * factor
    mixed = numerator / row_total + carried
    normed = mixed * lax.rsqrt(jnp.mean(mixed * mixed, axis=1, keepdims=True) + epsilon) * gain_row
    return normed.astype(jnp.bfloat16)


def compose(earlier, later):
    return (earlier[0] * later[0], later[0][:, None, None] * earlier[1] + later[1])


MESH = pl.DeviceIdType.MESH


def partner(me, flips, count):
    other, digit = me, 1
    while digit < count:
        if flips & digit:
            other = other + digit * (1 - 2 * ((me // digit) % 2))
        digit *= 2
    return other


def fused_kernel(
    count, blocks, q_ref, k_ref, v_ref, noise_ref, power_hbm, gain_hbm, out_ref,
    power_ref, gain_ref, small_done,
    q_all, k_all, v_all, outcome, fresh_mine, fresh_got,
    in_send, in_recv, out_send, out_recv, fresh_send, fresh_recv,
):
    rows = q_ref.shape[0]
    depth = gain_ref.shape[1]
    grouped = q_all.shape[0]
    total_rows = count * rows
    factor = depth ** (-0.5)
    me, now = lax.axis_index("space"), lax.axis_index("tm")
    peers = [partner(me, flips, count) for flips in range(count)]
    order = list(range(1, count))

    small = [
        pltpu.make_async_copy(held, here, small_done.at[index])
        for index, (held, here) in enumerate(
            ((power_hbm, power_ref), (gain_hbm, gain_ref))
        )
    ]
    for copy in small:
        copy.start()

    barrier = pltpu.get_barrier_semaphore()
    for flips in range(1, count):
        pl.semaphore_signal(barrier, inc=1, device_id={"space": peers[flips]}, device_id_type=MESH)
    for step in range(1, blocks):
        pl.semaphore_signal(
            barrier, inc=1, device_id={"tm": lax.rem(now + step, blocks)}, device_id_type=MESH
        )
    pl.semaphore_wait(barrier, count - 1 + blocks - 1)

    def lanes(head):
        return pl.ds(pl.multiple_of(head * depth, depth), depth)

    def part(device):
        return pl.ds(pl.multiple_of(device * rows, rows), rows)

    arrays = ((k_ref, k_all), (v_ref, v_all), (q_ref, q_all))
    def send_inputs(slot, others, chosen=range(len(arrays))):
        for which in chosen:
            source, target = arrays[which]
            for flips in others:
                pltpu.make_async_remote_copy(
                    src_ref=source.at[:, lanes(peers[flips] * grouped + slot)],
                    dst_ref=target.at[slot, part(me)],
                    send_sem=in_send.at[slot, which],
                    recv_sem=in_recv.at[slot, which],
                    device_id={"space": peers[flips]},
                    device_id_type=MESH,
                ).start()

    near, far = order[: count // 2 - 1], order[count // 2 - 1 :]
    send_inputs(0, far, (0,))
    for slot in range(grouped):
        send_inputs(slot, near)
    for slot in range(grouped):
        send_inputs(slot, far, range(1 if slot == 0 else 0, len(arrays)))
    for slot in range(grouped):
        for which, (source, target) in enumerate(arrays):
            pltpu.make_async_copy(
                source.at[:, lanes(me * grouped + slot)],
                target.at[slot, part(me)],
                in_recv.at[slot, which],
            ).start()

    def arrived(slot, which):
        whole = arrays[which][1].at[slot]
        pltpu.make_async_copy(whole, whole, in_recv.at[slot, which]).wait()

    def give_back(slot, flips):
        pltpu.make_async_remote_copy(
            src_ref=outcome.at[slot, part(peers[flips])],
            dst_ref=out_ref.at[:, lanes(me * grouped + slot)],
            send_sem=out_send.at[slot],
            recv_sem=out_recv.at[0],
            device_id={"space": peers[flips]},
            device_id_type=MESH,
        ).start()

    for copy in small:
        copy.wait()
    level = jnp.full((8, depth), noise_ref[0], jnp.int32).astype(jnp.float32)
    for slot in range(grouped):
        head = me * grouped + slot
        power = jnp.full((8, depth), power_ref[head], jnp.int32).astype(jnp.float32)
        rate = jnp.exp2(-(power * (0.25 + 1.75 * level / LEVELS)) / blocks)
        arrived(slot, 0)
        arrived(slot, 1)
        fresh = lax.dot_general(
            k_all[slot], v_all[slot], (((0,), (0,)), ((), ())), preferred_element_type=jnp.float32
        )
        fresh_mine[slot, 0:depth, :] = fresh / total_rows
        fresh_mine[slot, depth : depth + 8, :] = rate
        for step in range(1, blocks):
            pltpu.make_async_remote_copy(
                src_ref=fresh_mine.at[slot],
                dst_ref=fresh_got.at[slot, step - 1],
                send_sem=fresh_send.at[slot],
                recv_sem=fresh_recv.at[slot],
                device_id={"tm": lax.rem(now + step, blocks)},
                device_id_type=MESH,
            ).start()
        arrived(slot, 2)
        landed = fresh_got.at[slot]
        pltpu.make_async_copy(landed, landed, fresh_recv.at[slot]).wait()
        carried = jnp.zeros((depth, depth), jnp.float32)
        for step in range(blocks - 1, 0, -1):
            longer = (
                fresh_got[slot, step - 1, depth : depth + 1, :] * carried
                + fresh_got[slot, step - 1, 0:depth, :]
            )
            carried = jnp.where(now - step >= 0, longer, carried)
        state = (rate[0:1, :] * carried).astype(jnp.bfloat16)
        gain_row = gain_ref[pl.ds(head, 1), :]

        def attend(device):
            query = q_all[slot, part(device), :]
            scores = lax.dot_general(
                query, k_all[slot], (((1,), (1,)), ((), ())), preferred_element_type=jnp.float32
            ) * factor
            weights = jnp.exp(scores - jnp.max(scores, axis=1, keepdims=True))
            row_total = jnp.sum(weights, axis=1, keepdims=True)
            numerator = jnp.dot(
                weights.astype(jnp.bfloat16), v_all[slot], preferred_element_type=jnp.float32
            )
            before = jnp.dot(query, state, preferred_element_type=jnp.float32) * factor
            mixed = numerator / row_total + before
            scale = lax.rsqrt(jnp.mean(mixed * mixed, axis=1, keepdims=True) + epsilon)
            outcome[slot, part(device), :] = (mixed * scale * gain_row).astype(jnp.bfloat16)

        for flips in order:
            attend(peers[flips])
            if slot == grouped - 1:
                give_back(slot, flips)
        attend(me)
        if slot == grouped - 2:
            for earlier in range(slot + 1):
                for flips in far + near:
                    give_back(earlier, flips)
        pltpu.make_async_copy(
            outcome.at[slot, part(me)], out_ref.at[:, lanes(head)], out_recv.at[0]
        ).start()

    for slot in range(grouped):
        for which in range(len(arrays)):
            sent = arrays[which][1].at[slot, pl.ds(0, total_rows - rows)]
            pltpu.make_async_copy(sent, sent, in_send.at[slot, which]).wait()
        landed = fresh_got.at[slot]
        pltpu.make_async_copy(landed, landed, fresh_send.at[slot]).wait()
        returned = outcome.at[slot, pl.ds(0, total_rows - rows)]
        pltpu.make_async_copy(returned, returned, out_send.at[slot]).wait()
    pltpu.make_async_copy(out_ref, out_ref, out_recv.at[0]).wait()


def fused(queries, key_rows, value_rows, noise_level, decay_power, head_gain):
    count, blocks = lax.axis_size("space"), lax.axis_size("tm")
    rows, width = queries.shape[1:]
    heads_total, depth = head_gain.shape
    grouped = heads_total // count
    held = [
        pltpu.with_memory_space_constraint(operand, pltpu.HBM)
        for operand in (queries[0], key_rows[0], value_rows[0], decay_power, head_gain)
    ]
    gathered = pltpu.VMEM((grouped, count * rows, depth), jnp.bfloat16)
    dma = pltpu.SemaphoreType.DMA
    out = pl.pallas_call(
        functools.partial(fused_kernel, count, blocks),
        out_shape=jax.ShapeDtypeStruct((rows, width), jnp.bfloat16),
        in_specs=[pl.BlockSpec(memory_space=pl.ANY)] * 3
        + [pl.BlockSpec(memory_space=pltpu.SMEM)]
        + [pl.BlockSpec(memory_space=pl.ANY)] * 2,
        out_specs=pl.BlockSpec(memory_space=pl.ANY),
        scratch_shapes=[
            pltpu.SMEM(decay_power.shape, jnp.int32),
            pltpu.VMEM(head_gain.shape, jnp.float32),
            dma((2,)),
            gathered,
            gathered,
            gathered,
            gathered,
            pltpu.VMEM((grouped, depth + 8, depth), jnp.float32),
            pltpu.VMEM((grouped, blocks - 1, depth + 8, depth), jnp.float32),
            dma((grouped, 3)),
            dma((grouped, 3)),
            dma((grouped,)),
            dma((1,)),
            dma((grouped,)),
            dma((grouped,)),
        ],
        compiler_params=pltpu.CompilerParams(collective_id=0, has_side_effects=True, vmem_limit_bytes=VMEM_GRANT),
        name="heads_exchange",
    )(*held[:3], noise_level, *held[3:])
    return out[None]


def body(queries, key_rows, value_rows, noise_level, decay_power, head_gain):
    heads_total = decay_power.shape[0]
    depth = head_gain.shape[1]
    local_rows = queries.shape[1]
    quarters = lax.axis_size("space") // HGROUPS
    grouped = heads_total // HGROUPS
    query_items = spread_items(queries[0], quarters, heads_total, depth)
    keys_sent = copied_items(key_rows[0], quarters, heads_total, depth)
    values_sent = copied_items(value_rows[0], quarters, heads_total, depth)
    query_got, keys_got, values_got = (
        lax.all_to_all(query_items, "space", split_axis=0, concat_axis=1, tiled=True),
        lax.all_to_all(keys_sent, "space", split_axis=0, concat_axis=1, tiled=True),
        lax.all_to_all(values_sent, "space", split_axis=0, concat_axis=1, tiled=True),
    )
    key_count = keys_got.shape[1]
    fresh = (
        jnp.einsum("inh,ine->ihe", keys_got, values_got, preferred_element_type=jnp.float32)
        / key_count
    )
    group_index = lax.axis_index("space") % HGROUPS
    powers = lax.dynamic_slice_in_dim(decay_power, group_index * grouped, grouped).astype(
        jnp.float32
    )
    level_now = noise_level[0].astype(jnp.float32)
    block_count = lax.axis_size("tm")
    rate = jnp.exp2(-(powers * (0.25 + 1.75 * level_now / LEVELS)) / block_count)
    zeros_state = jnp.zeros_like(fresh)
    unused_rate, before = carried_in(
        (rate, fresh), "tm", compose, (jnp.ones_like(rate), zeros_state)
    )
    state = (rate[:, None, None] * before).astype(jnp.bfloat16)
    gain_rows = lax.dynamic_slice_in_dim(head_gain, group_index * grouped, grouped)
    outcome = lax.map(attend_head, (query_got, keys_got, values_got, state, gain_rows))
    returned = lax.all_to_all(outcome, "space", split_axis=1, concat_axis=0, tiled=True)
    part_rows = local_rows // quarters
    restored = returned.reshape(quarters, heads_total, part_rows, depth).transpose(0, 2, 1, 3)
    return restored.reshape(1, local_rows, heads_total * depth)


def solution(mesh):
    in_specs = (
        P("tm", "space", None),
        P("tm", "space", None),
        P("tm", "space", None),
        P("tm"),
        P(),
        P(),
    )
    out_specs = P("tm", "space", None)
    step = fused if mesh.shape["space"] == HGROUPS else body
    return jax.shard_map(step, mesh=mesh, in_specs=in_specs, out_specs=out_specs, check_vma=False)
```
